32 devices in a mesh: groups: 2 (over y), shots: 4 (over z), dom: 2 (over x), sub: 2 (over core).
Axes of the slice: x: 2, y: 2, z: 4, core: 2. Of those that a mesh axis runs over, the one named last changes fastest.
Arguments:
- velocity: float32 [64, 16, 256], P(('groups', 'shots'), 'dom', 'sub'), parts along dimension 0, may hold values from 0.15 to 0.4
- wave_prev: bfloat16 [8, 32, 16, 256], P(('groups', 'shots'), None, 'dom', 'sub'), parts along dimension 0, may hold values from -6 to 6
- wave_now: bfloat16 [8, 32, 16, 256], P(('groups', 'shots'), None, 'dom', 'sub'), parts along dimension 0, may hold values from -6 to 6
- adj_next: bfloat16 [8, 32, 16, 256], P(('groups', 'shots'), None, 'dom', 'sub'), parts along dimension 0, may hold values from -6 to 6
- adj_now: bfloat16 [8, 32, 16, 256], P(('groups', 'shots'), None, 'dom', 'sub'), parts along dimension 0, may hold values from -6 to 6
- sponge: int32 [32, 16, 256], P(None, 'dom', 'sub'), may hold values 0 or 1
- wavelet: float32 [8, 6], P(('groups', 'shots')), parts along dimension 0, may hold values from -12 to 12
- src_pos: int32 [8], P(('groups', 'shots')), parts along dimension 0, may hold values from 0 to 4095
- rec_pos: int32 [8, 256], P(('groups', 'shots')), parts along dimension 0, may hold values from 0 to 4095
- observed: float32 [8, 4, 256], P(('groups', 'shots')), parts along dimension 0, may hold values from -6 to 6
Outputs:
- direction: float32 [64, 16, 256], P(('groups', 'shots'), 'dom', 'sub'), parts along dimension 0
- wave_out: float32 [8, 32, 16, 256], P(('groups', 'shots'), None, 'dom', 'sub'), parts along dimension 0
The draws below stay inside these ranges and needn't reach their ends.
There are 2 independent parts, one for each index of `groups`. The reference program is written for one: setup_inputs(seed, part) draws one part's arguments, and reference() takes and returns one part's arrays. A program takes and returns all parts, laid end to end along the dimension named above; an argument that names none is the same for every part. Nothing has to cross between parts.
Inputs may be any that keep to these rules, and one draw needn't show every extreme that they name: `src_pos`: a horizontal position x * 256 + y on the grid. `rec_pos`: horizontal positions x * 256 + y on the grid, possibly repeated.
All inputs are finite; a program needn't handle non-finite values. Where the reference program divides by a largest or mean magnitude, that divisor is 1e-20 or more. No bound on the sum of `sponge` on one device may be relied on, other than what follows from the above.
Results may differ from the reference program's by a relative error of at most 0.0003.
Values sent between devices are 32-bit elements; how exact they have to be, the bound alone decides.
A program may use at most 64 MiB of HBM per device.

```python
import math
import jax
import jax.numpy as jnp
from jax import lax

NZ = 32
NREC = 256
NF = 4
NFIN = 2
SHOTS = 4
NX = 16
NY = 256


def touch_ends(result, stream_key, smallest, largest):
    longest = result.shape.index(max(result.shape))
    spots = []
    for shift in (0, 1):
        where = [jax.random.randint(jax.random.fold_in(stream_key, axis), (), 0, length) for axis, length in enumerate(result.shape)]
        where[longest] = (where[longest] + shift) % result.shape[longest]
        spots.append(tuple(where))
    return result.at[spots[0]].set(smallest).at[spots[1]].set(largest)


def steps_of(key, shape, split, low, top_value):
    level, own = 1.0, jax.random.fold_in(key, 6)
    for dim, blocks in split:
        draws = jnp.exp(jax.random.uniform(jax.random.fold_in(own, dim), (blocks,), jnp.float32, low / len(split), top_value / len(split)))
        level = level * jnp.repeat(draws, shape[dim] // blocks).reshape([-1 if axis == dim else 1 for axis in range(len(shape))])
    return level


def bell_draw(own_key, shape, spread, most, pieces=(), dtype=jnp.bfloat16):
    array = jax.random.normal(own_key, shape, jnp.float32) * spread
    if len(pieces) > 0:
        array = steps_of(own_key, shape, pieces, -0.22, 0.18) * array
    return jnp.clip(array, min=-most, max=most).astype(dtype)


def setup_inputs(seed: int = 0, part: int = 0) -> dict:
    keys = jax.random.split(jax.random.key(seed), 11)
    part_splits = jax.random.split(jax.random.fold_in(keys[10], part), 11)
    return {
        "velocity": jnp.clip(jnp.exp(math.log(0.4) - 0.98082923 * jax.random.uniform(part_splits[0], (NZ, NX, NY), jnp.float32) ** steps_of(part_splits[0], (NZ, NX, NY), ((0, 4), (1, 2), (2, 2)), -0.2, 0.2)), 0.15, 0.4),
        "wave_prev": bell_draw(part_splits[1], (SHOTS, NZ, NX, NY), 1.0, 6.0, ((0, 4), (2, 2), (3, 2))),
        "wave_now": bell_draw(part_splits[2], (SHOTS, NZ, NX, NY), 1.0, 6.0, ((0, 4), (2, 2), (3, 2))),
        "adj_next": bell_draw(part_splits[3], (SHOTS, NZ, NX, NY), 1.0, 6.0, ((0, 4), (2, 2), (3, 2))),
        "adj_now": bell_draw(part_splits[4], (SHOTS, NZ, NX, NY), 1.0, 6.0, ((0, 4), (2, 2), (3, 2))),
        "sponge": touch_ends((jax.random.randint(keys[5], (NZ, NX, NY), 0, 4) < 1).astype(jnp.int32), jax.random.fold_in(keys[5], 1), 0, 1),
        "wavelet": bell_draw(part_splits[6], (SHOTS, NF + NFIN), 3.0, 12.0, ((0, 4),), jnp.float32),
        "src_pos": touch_ends(jax.random.randint(part_splits[7], (SHOTS,), 0, NX * NY), jax.random.fold_in(part_splits[7], 1), 0, (NX * NY) - 1).astype(jnp.int32),
        "rec_pos": touch_ends(jax.random.randint(part_splits[8], (SHOTS, NREC), 0, NX * NY), jax.random.fold_in(part_splits[8], 1), 0, (NX * NY) - 1).astype(jnp.int32),
        "observed": bell_draw(part_splits[9], (SHOTS, NF, NREC), 1.0, 6.0, ((0, 4),), jnp.float32),
    }


coeffs = (-205.0 / 72.0, 8.0 / 5.0, -1.0 / 5.0, 8.0 / 315.0, -1.0 / 560.0)
damp_rate = 0.2
step_rate = 0.1
floor_share = 0.5
src_depth = 2
rec_depth = 1
reach = 4


def laplace(padded, depth, rows, cols):
    z0, x0, y0 = reach, reach, reach
    total = (3.0 * coeffs[0]) * padded[z0:z0 + depth, x0:x0 + rows, y0:y0 + cols]
    for offset in range(1, 5):
        pair = padded[z0 + offset:z0 + offset + depth, x0:x0 + rows, y0:y0 + cols]
        pair = pair + padded[z0 - offset:z0 - offset + depth, x0:x0 + rows, y0:y0 + cols]
        pair = pair + padded[z0:z0 + depth, x0 + offset:x0 + offset + rows, y0:y0 + cols]
        pair = pair + padded[z0:z0 + depth, x0 - offset:x0 - offset + rows, y0:y0 + cols]
        pair = pair + padded[z0:z0 + depth, x0:x0 + rows, y0 + offset:y0 + offset + cols]
        pair = pair + padded[z0:z0 + depth, x0:x0 + rows, y0 - offset:y0 - offset + cols]
        total = total + coeffs[offset] * pair
    return total


def advance(now, before, kappa, damp, plane, level):
    padded = jnp.pad(now, reach)
    lap = laplace(padded, now.shape[0], now.shape[1], now.shape[2])
    numer = 2.0 * now - (1.0 - damp) * before + kappa * lap
    numer = numer.at[level].add(plane)
    return numer / (1.0 + damp)


def place(positions, values):
    flat = jnp.zeros((NX * NY,), jnp.float32).at[positions].add(values)
    return flat.reshape(NX, NY)


def forward(prev, now, kappa, damp, amps, spot):
    states = [prev.astype(jnp.float32), now.astype(jnp.float32)]
    for step in range(NF):
        plane = place(spot[None], amps[step][None])
        states.append(advance(states[-1], states[-2], kappa, damp, plane, src_depth))
    return states


def reference(velocity, wave_prev, wave_now, adj_next, adj_now, sponge, wavelet, src_pos, rec_pos, observed):
    kappa = velocity * velocity
    damp = damp_rate * sponge.astype(jnp.float32)

    def one_shot(carry, items):
        grad_total, illum_total = carry
        prev, now, lam_after, lam_now, amps, spot, receivers, recorded = items
        states = forward(prev, now, kappa, damp, amps, spot)
        lam_after = lam_after.astype(jnp.float32)
        lam_now = lam_now.astype(jnp.float32)
        grad = jnp.zeros_like(kappa)
        for level in range(NF, 0, -1):
            trace = states[level + 1][rec_depth].reshape(-1)[receivers]
            resid = trace - recorded[level - 1]
            plane = place(receivers, resid)
            lam_before = advance(lam_now, lam_after, kappa, damp, plane, rec_depth)
            lower = level - 1
            accel = states[lower + 2] - 2.0 * states[lower + 1] + states[lower]
            grad = grad + lam_before * accel
            lam_after, lam_now = lam_now, lam_before
        illum = jnp.zeros_like(kappa)
        for level in range(1, NF + 1):
            illum = illum + states[level + 1] * states[level + 1]
        return (grad_total + grad, illum_total + illum), None

    zeros = jnp.zeros_like(kappa)
    (gradient, illumination), _ = lax.scan(one_shot, (zeros, zeros),
                                           (wave_prev, wave_now, adj_next, adj_now, wavelet, src_pos, rec_pos, observed))
    precond = gradient / (illumination + floor_share * SHOTS)
    peak = jnp.max(jnp.abs(precond))
    direction = precond / (peak + 1e-6)
    updated = velocity * (1.0 - step_rate * direction)
    kappa_new = updated * updated

    def final_shot(items):
        prev, now, amps, spot = items
        states = forward(prev, now, kappa, damp, amps, spot)
        before, current = states[-2], states[-1]
        for step in range(NFIN):
            plane = place(spot[None], amps[NF + step][None])
            nxt = advance(current, before, kappa_new, damp, plane, src_depth)
            before, current = current, nxt
        return current

    wave_out = lax.map(final_shot, (wave_prev, wave_now, wavelet, src_pos))
    return direction, wave_out
```

```python
import functools

import jax
import jax.numpy as jnp
import numpy as np
from jax import lax
from jax.experimental import pallas as pl
from jax.experimental.pallas import tpu as pltpu
from jax.sharding import PartitionSpec as P

NF = 4
NFIN = 2

coeffs = (-205.0 / 72.0, 8.0 / 5.0, -1.0 / 5.0, 8.0 / 315.0, -1.0 / 560.0)
damp_rate = 0.2
step_rate = 0.1
floor_share = 0.5
src_depth = 2
rec_depth = 1
reach = 4

MESH = pl.DeviceIdType.MESH
F32 = jnp.float32
BF16 = jnp.bfloat16


def band(size, period):
    full = np.zeros((size, size), np.float64)
    for row in range(size):
        for k in range(1, reach + 1):
            for col in (row - k, row + k):
                if 0 <= col < size and col // period == row // period:
                    full[row, col] = coeffs[k]
    high = full.astype(np.float32).astype(BF16)
    low = (full - high.astype(np.float64)).astype(np.float32).astype(BF16)
    return high, low


def split(value):
    high = value.astype(BF16)
    low = (value - high.astype(F32)).astype(BF16)
    return high, low


def copies_needed(shots, dom, sub):
    fields = 5 * ((dom - 1) + dom * (sub - 1))
    slabs = 2 * (shots * dom * sub)
    return fields + slabs + shots


def kernel(
    sizes,
    vel_ref, prev_ref, now_ref, adjn_ref, adj_ref, sponge_ref, amp_ref, src_ref, rec_ref, obs_ref,
    bh_ref, bl_ref, kh_ref, kl_ref,
    dir_ref, out_ref,
    U, L, V, SP, IV, QV, KP, ACC, PC, OB, CNT, GI, GR, ss, rs,
):
    shots, dom, sub, depth, rows, cols, owned, zb = sizes
    X, Y = dom * rows, sub * cols
    s = lax.axis_index("shots")
    d = lax.axis_index("dom")
    c = lax.axis_index("sub")
    counts = {"shots": shots, "dom": dom, "sub": sub}
    me = {"shots": s, "dom": d, "sub": c}
    tickets = [0]
    sent = []

    def peer(axis, j):
        return lax.rem(me[axis] + j, counts[axis])

    def source(axis, j):
        return lax.rem(me[axis] + (counts[axis] - j), counts[axis])

    def xs(i):
        return pl.ds(pl.multiple_of(i * rows, rows), rows)

    def ys(i):
        return pl.ds(pl.multiple_of(i * cols, cols), cols)

    def send(src, dst, axis, j):
        idx = tickets[0]
        tickets[0] += 1
        copy = pltpu.make_async_remote_copy(
            src_ref=src, dst_ref=dst, send_sem=ss.at[idx], recv_sem=rs.at[idx],
            device_id={axis: peer(axis, j)}, device_id_type=MESH,
        )
        copy.start()
        sent.append(copy)
        return idx

    def arrived(idx, dst, axis):
        pltpu.make_async_remote_copy(
            src_ref=dst, dst_ref=dst, send_sem=ss.at[idx], recv_sem=rs.at[idx],
            device_id={axis: peer(axis, 1)}, device_id_type=MESH,
        ).wait_recv()

    def field_send(place):
        hops = [(i, send(place(d, c), place(d, c), "dom", i)) for i in range(1, dom)]
        cross = [(0, k, send(place(d, c), place(d, c), "sub", k)) for k in range(1, sub)]
        return hops, cross

    def field_relay(place, state):
        hops, cross = state
        for i, idx in hops:
            here = place(source("dom", i), c)
            arrived(idx, here, "dom")
            cross += [(i, k, send(here, here, "sub", k)) for k in range(1, sub)]

    def field_done(place, state):
        for i, k, idx in state[1]:
            arrived(idx, place(source("dom", i), source("sub", k)), "sub")

    def slab_send(place, first, second):
        own = place({"shots": s, "dom": d}, c)
        state = {
            "one": [(i, send(own, own, first, i)) for i in range(1, counts[first])],
            "two": [(0, j, send(own, own, second, j)) for j in range(1, counts[second])],
            "cross": [(0, 0, k, send(own, own, "sub", k)) for k in range(1, sub)],
        }
        return state

    def slab_relay(place, state, first, second):
        for i, idx in state["one"]:
            here = place({first: source(first, i), second: me[second]}, c)
            arrived(idx, here, first)
            state["two"] += [(i, j, send(here, here, second, j)) for j in range(1, counts[second])]
            state["cross"] += [(i, 0, k, send(here, here, "sub", k)) for k in range(1, sub)]
        for i, j, idx in state["two"]:
            here = place({first: source(first, i), second: source(second, j)}, c)
            arrived(idx, here, second)
            state["cross"] += [(i, j, k, send(here, here, "sub", k)) for k in range(1, sub)]

    def slab_done(place, state, first, second):
        for i, j, k, idx in state["cross"]:
            arrived(idx, place({first: source(first, i), second: source(second, j)}, source("sub", k)), "sub")

    def in_field(ref, n):
        return lambda i, k: ref.at[n, pl.ds(reach, depth), xs(i), ys(k)]

    def in_whole(ref):
        return lambda i, k: ref.at[:, xs(i), ys(k)]

    def in_slab(ref):
        return lambda at, k: ref.at[pl.ds(at["shots"] * owned, owned), xs(at["dom"]), ys(k)]

    barrier = pltpu.get_barrier_semaphore()
    for axis, count in counts.items():
        for j in range(1, count):
            pl.semaphore_signal(barrier, inc=1, device_id={axis: peer(axis, j)}, device_id_type=MESH)

    own_x, own_y = xs(d), ys(c)
    V[pl.ds(s * owned, owned), own_x, own_y] = vel_ref[...]
    U[1, pl.ds(reach, depth), own_x, own_y] = now_ref[0].astype(F32)
    U[0, pl.ds(reach, depth), own_x, own_y] = prev_ref[0].astype(F32)
    SP[:, own_x, own_y] = sponge_ref[...].astype(F32)
    L[1, pl.ds(reach, depth), own_x, own_y] = adj_ref[0].astype(F32)
    L[0, pl.ds(reach, depth), own_x, own_y] = adjn_ref[0].astype(F32)

    pl.semaphore_wait(barrier, sum(counts.values()) - 3)

    vel_state = slab_send(in_slab(V), "dom", "shots")
    now_state = field_send(in_field(U, 1))
    sp_state = field_send(in_whole(SP))
    prev_state = field_send(in_field(U, 0))
    adj_state = field_send(in_field(L, 1))
    adjn_state = field_send(in_field(L, 0))

    edge = jnp.zeros((reach, X, Y), F32)
    for ref in (U, L):
        for n in range(ref.shape[0]):
            ref[n, 0:reach] = edge
            ref[n, reach + depth : 2 * reach + depth] = edge
    pos = rec_ref[...]
    row_of = jnp.zeros_like(pos)
    for x in range(1, X):
        row_of = row_of + (pos >= x * Y).astype(jnp.int32)
    col_of = pos - row_of * Y
    nrec = pos.shape[1]
    x_hot = (lax.broadcasted_iota(jnp.int32, (X, nrec), 0) == row_of).astype(F32)
    y_hot = (lax.broadcasted_iota(jnp.int32, (Y, nrec), 0) == col_of).astype(F32).astype(BF16)

    def spread(lhs):
        return lax.dot_general(lhs, y_hot, (((1,), (1,)), ((), ())), preferred_element_type=F32)

    CNT[...] = spread(x_hot.astype(BF16))
    for n in range(NF):
        vals = x_hot * obs_ref[0, n : n + 1, :]
        a, rest = split(vals)
        b, rest2 = split(vals - a.astype(F32))
        del rest
        OB[n] = spread(a) + spread(b) + spread(rest2)
    flat = lax.broadcasted_iota(jnp.int32, (X, Y), 0) * Y + lax.broadcasted_iota(jnp.int32, (X, Y), 1)
    src_hot = (flat == src_ref[0]).astype(F32)

    slab_relay(in_slab(V), vel_state, "dom", "shots")
    field_relay(in_field(U, 1), now_state)
    field_relay(in_whole(SP), sp_state)
    field_relay(in_field(U, 0), prev_state)
    slab_done(in_slab(V), vel_state, "dom", "shots")
    field_done(in_whole(SP), sp_state)
    for z in range(depth):
        damp = damp_rate * SP[z]
        inv = 1.0 / (1.0 + damp)
        IV[z] = inv
        QV[z] = (1.0 - damp) * inv
        vel = V[z]
        KP[z] = vel * vel * inv
    field_done(in_field(U, 1), now_state)
    field_done(in_field(U, 0), prev_state)

    def lateral(ref, n):
        for b in range(depth // zb):
            lo = reach + b * zb
            u = ref[n, lo : lo + zb].reshape(zb * X, Y)
            uh, ul = split(u)
            acc = jnp.dot(uh, bh_ref[...], preferred_element_type=F32)
            acc = acc + jnp.dot(kh_ref[...], uh, preferred_element_type=F32)
            acc = acc + jnp.dot(uh, bl_ref[...], preferred_element_type=F32)
            acc = acc + jnp.dot(ul, bh_ref[...], preferred_element_type=F32)
            acc = acc + jnp.dot(kl_ref[...], uh, preferred_element_type=F32)
            acc = acc + jnp.dot(kh_ref[...], ul, preferred_element_type=F32)
            ACC[b * zb : (b + 1) * zb] = acc.reshape(zb, X, Y)

    def level(ref, n, z, xr, yr, plane):
        mid = ref[n, reach + z, xr, yr]
        lap = ACC[z, xr, yr] + (3.0 * coeffs[0]) * mid
        for k in range(1, reach + 1):
            lap = lap + coeffs[k] * (ref[n, reach + z + k, xr, yr] + ref[n, reach + z - k, xr, yr])
        inv = IV[z, xr, yr]
        drive = 2.0 * mid if plane is None else 2.0 * mid + plane
        return inv * drive - QV[z, xr, yr] * ref[n - 1, reach + z, xr, yr] + KP[z, xr, yr] * lap

    whole_x, whole_y = slice(None), slice(None)

    def advance(ref, n, plane, at):
        lateral(ref, n)
        for z in range(depth):
            ref[n + 1, reach + z] = level(ref, n, z, whole_x, whole_y, plane if z == at else None)

    for n in range(NF):
        advance(U, n + 1, src_hot * amp_ref[0, n], src_depth)
        if n == 0:
            field_relay(in_field(L, 1), adj_state)
        if n == 1:
            field_relay(in_field(L, 0), adjn_state)
    field_done(in_field(L, 1), adj_state)
    field_done(in_field(L, 0), adjn_state)

    for n in range(NF, 0, -1):
        plane = CNT[...] * U[n + 1, reach + rec_depth] - OB[n - 1]
        advance(L, NF + 1 - n, plane, rec_depth)

    for z in range(depth):
        at = (reach + z, own_x, own_y)
        u = [U[(n,) + at] for n in range(NF + 2)]
        grad = None
        illum = None
        for n in range(NF):
            term = L[(NF + 1 - n,) + at] * (u[n + 2] - 2.0 * u[n + 1] + u[n])
            grad = term if grad is None else grad + term
            square = u[n + 2] * u[n + 2]
            illum = square if illum is None else illum + square
        GI[0, z] = grad
        GI[1, z] = illum

    parts = []
    for j in range(1, shots):
        to = peer("shots", j)
        parts.append(send(GI.at[:, pl.ds(to * owned, owned)], GR.at[j - 1], "shots", j))
    lateral(U, NF + 1)
    total = GI[:, pl.ds(s * owned, owned)]
    for j in range(1, shots):
        arrived(parts[j - 1], GR.at[j - 1], "shots")
        total = total + GR[j - 1]
    mine = total[0] / (total[1] + floor_share * shots)
    PC[pl.ds(s * owned, owned), own_x, own_y] = mine
    pc_state = slab_send(in_slab(PC), "shots", "dom")
    slab_relay(in_slab(PC), pc_state, "shots", "dom")
    slab_done(in_slab(PC), pc_state, "shots", "dom")
    top = jnp.abs(PC[0])
    for z in range(1, depth):
        top = jnp.maximum(top, jnp.abs(PC[z]))
    peak = jnp.max(jnp.max(top, axis=0, keepdims=True), axis=1, keepdims=True)
    scale = 1.0 / (peak + 1e-06)
    dir_ref[...] = mine * scale
    for z in range(depth):
        updated = V[z] * (1.0 - step_rate * (PC[z] * scale))
        KP[z] = updated * updated * IV[z]
    for n in range(NFIN):
        plane = src_hot * amp_ref[0, NF + n]
        if n > 0:
            lateral(U, NF + 1 + n)
        if n < NFIN - 1:
            for z in range(depth):
                U[NF + 2 + n, reach + z] = level(
                    U, NF + 1 + n, z, whole_x, whole_y, plane if z == src_depth else None
                )
        else:
            for z in range(depth):
                out_ref[0, z] = level(U, NF + 1 + n, z, own_x, own_y, None)
            ACC[0] = plane * IV[src_depth]
            out_ref[0, src_depth] += ACC[0, own_x, own_y]
    for copy in sent:
        copy.wait_send()


def solution(mesh):
    shots, dom, sub = mesh.shape["shots"], mesh.shape["dom"], mesh.shape["sub"]

    def shards(velocity, wave_prev, wave_now, adj_next, adj_now, sponge, wavelet, src_pos, rec_pos, observed):
        depth, rows, cols = sponge.shape
        owned = velocity.shape[0]
        X, Y = dom * rows, sub * cols
        zb = min(depth, max(1, 256 // X))
        bh, bl = band(Y, Y)
        kh, kl = band(zb * X, X)
        vm = pl.BlockSpec(memory_space=pltpu.VMEM)
        sm = pl.BlockSpec(memory_space=pltpu.SMEM)
        whole = pltpu.VMEM((depth, X, Y), F32)
        n_sems = copies_needed(shots, dom, sub)
        return tuple(pl.pallas_call(
            functools.partial(kernel, (shots, dom, sub, depth, rows, cols, owned, zb)),
            out_shape=(
                jax.ShapeDtypeStruct((owned, rows, cols), F32),
                jax.ShapeDtypeStruct((1, depth, rows, cols), F32),
            ),
            in_specs=[vm] * 6 + [sm, sm] + [vm] * 6,
            out_specs=(vm, vm),
            scratch_shapes=[
                pltpu.VMEM((NF + NFIN + 1, depth + 2 * reach, X, Y), F32),
                pltpu.VMEM((NF + 2, depth + 2 * reach, X, Y), F32),
                whole, whole, whole, whole, whole, whole, whole,
                pltpu.VMEM((NF, X, Y), F32),
                pltpu.VMEM((X, Y), F32),
                pltpu.VMEM((2, depth, rows, cols), F32),
                pltpu.VMEM((max(1, shots - 1), 2, owned, rows, cols), F32),
                pltpu.SemaphoreType.DMA((n_sems,)),
                pltpu.SemaphoreType.DMA((n_sems,)),
            ],
            compiler_params=pltpu.CompilerParams(
                collective_id=0, has_side_effects=True, vmem_limit_bytes=56 * 1024 * 1024
            ),
        )(velocity, wave_prev, wave_now, adj_next, adj_now, sponge, wavelet, src_pos, rec_pos, observed,
          jnp.asarray(bh), jnp.asarray(bl), jnp.asarray(kh), jnp.asarray(kl)))

    return jax.shard_map(
        shards,
        mesh=mesh,
        in_specs=(
            P(("groups", "shots"), "dom", "sub"),
            P(("groups", "shots"), None, "dom", "sub"),
            P(("groups", "shots"), None, "dom", "sub"),
            P(("groups", "shots"), None, "dom", "sub"),
            P(("groups", "shots"), None, "dom", "sub"),
            P(None, "dom", "sub"),
            P(("groups", "shots"), None),
            P(("groups", "shots")),
            P(("groups", "shots"), None),
            P(("groups", "shots"), None, None),
        ),
        out_specs=(
            P(("groups", "shots"), "dom", "sub"),
            P(("groups", "shots"), None, "dom", "sub"),
        ),
        check_vma=False,
    )
```

```python
import functools

import jax
import jax.numpy as jnp
import numpy as np
from jax import lax
from jax.experimental import pallas as pl
from jax.experimental.pallas import tpu as pltpu
from jax.sharding import PartitionSpec as P

NF = 4
NFIN = 2

coeffs = (-205.0 / 72.0, 8.0 / 5.0, -1.0 / 5.0, 8.0 / 315.0, -1.0 / 560.0)
damp_rate = 0.2
step_rate = 0.1
floor_share = 0.5
src_depth = 2
rec_depth = 1
reach = 4

MESH = pl.DeviceIdType.MESH
F32 = jnp.float32
BF16 = jnp.bfloat16


def band(size, period):
    full = np.zeros((size, size), np.float64)
    for row in range(size):
        for k in range(1, reach + 1):
            for col in (row - k, row + k):
                if 0 <= col < size and col // period == row // period:
                    full[row, col] = coeffs[k]
    high = full.astype(np.float32).astype(BF16)
    low = (full - high.astype(np.float64)).astype(np.float32).astype(BF16)
    return high, low


def split(value):
    high = value.astype(BF16)
    low = (value - high.astype(F32)).astype(BF16)
    return high, low


def copies_needed(shots, dom, sub):
    fields = 5 * ((dom - 1) + dom * (sub - 1))
    slabs = 2 * (shots * dom * sub)
    return fields + slabs + 2 * shots


def kernel(
    sizes,
    vel_ref, prev_ref, now_ref, adjn_ref, adj_ref, sponge_ref, amp_ref, src_ref, rec_ref, obs_ref,
    bh_ref, bl_ref, kh_ref, kl_ref,
    both_ref,
    U, L, V, SP, IV, QV, KP, ACC, PC, OB, CNT, GI, GR, ss, rs,
):
    shots, dom, sub, depth, rows, cols, owned, zb = sizes
    X, Y = dom * rows, sub * cols
    s = lax.axis_index("shots")
    d = lax.axis_index("dom")
    c = lax.axis_index("sub")
    counts = {"shots": shots, "dom": dom, "sub": sub}
    me = {"shots": s, "dom": d, "sub": c}
    tickets = [0]
    sent = []

    def peer(axis, j):
        return lax.rem(me[axis] + j, counts[axis])

    def source(axis, j):
        return lax.rem(me[axis] + (counts[axis] - j), counts[axis])

    def xs(i):
        return pl.ds(pl.multiple_of(i * rows, rows), rows)

    def ys(i):
        return pl.ds(pl.multiple_of(i * cols, cols), cols)

    def send(src, dst, axis, j):
        idx = tickets[0]
        tickets[0] += 1
        copy = pltpu.make_async_remote_copy(
            src_ref=src, dst_ref=dst, send_sem=ss.at[idx], recv_sem=rs.at[idx],
            device_id={axis: peer(axis, j)}, device_id_type=MESH,
        )
        copy.start()
        sent.append(copy)
        return idx

    def arrived(idx, dst, axis):
        pltpu.make_async_remote_copy(
            src_ref=dst, dst_ref=dst, send_sem=ss.at[idx], recv_sem=rs.at[idx],
            device_id={axis: peer(axis, 1)}, device_id_type=MESH,
        ).wait_recv()

    def field_send(place):
        hops = [(i, send(place(d, c), place(d, c), "dom", i)) for i in range(1, dom)]
        cross = [(0, k, send(place(d, c), place(d, c), "sub", k)) for k in range(1, sub)]
        return hops, cross

    def field_relay(place, state):
        hops, cross = state
        for i, idx in hops:
            here = place(source("dom", i), c)
            arrived(idx, here, "dom")
            cross += [(i, k, send(here, here, "sub", k)) for k in range(1, sub)]

    def field_done(place, state):
        for i, k, idx in state[1]:
            arrived(idx, place(source("dom", i), source("sub", k)), "sub")

    def slab_send(place, first, second):
        own = place({"shots": s, "dom": d}, c)
        state = {
            "one": [(i, send(own, own, first, i)) for i in range(1, counts[first])],
            "two": [(0, j, send(own, own, second, j)) for j in range(1, counts[second])],
            "cross": [(0, 0, k, send(own, own, "sub", k)) for k in range(1, sub)],
        }
        return state

    def slab_relay(place, state, first, second):
        for i, idx in state["one"]:
            here = place({first: source(first, i), second: me[second]}, c)
            arrived(idx, here, first)
            state["two"] += [(i, j, send(here, here, second, j)) for j in range(1, counts[second])]
            state["cross"] += [(i, 0, k, send(here, here, "sub", k)) for k in range(1, sub)]

    def slab_relay_two(place, state, first, second):
        for i, j, idx in state["two"]:
            here = place({first: source(first, i), second: source(second, j)}, c)
            arrived(idx, here, second)
            state["cross"] += [(i, j, k, send(here, here, "sub", k)) for k in range(1, sub)]

    def slab_done(place, state, first, second):
        for i, j, k, idx in state["cross"]:
            arrived(idx, place({first: source(first, i), second: source(second, j)}, source("sub", k)), "sub")

    def in_field(ref, n):
        return lambda i, k: ref.at[n, pl.ds(reach, depth), xs(i), ys(k)]

    def in_whole(ref):
        return lambda i, k: ref.at[:, xs(i), ys(k)]

    def in_slab(ref):
        return lambda at, k: ref.at[pl.ds(at["shots"] * owned, owned), xs(at["dom"]), ys(k)]

    def lateral(ref, n):
        for b in range(depth // zb):
            lo = reach + b * zb
            u = ref[n, lo : lo + zb].reshape(zb * X, Y)
            uh, ul = split(u)
            acc = jnp.dot(uh, bh_ref[...], preferred_element_type=F32)
            acc = acc + jnp.dot(kh_ref[...], uh, preferred_element_type=F32)
            acc = acc + jnp.dot(uh, bl_ref[...], preferred_element_type=F32)
            acc = acc + jnp.dot(ul, bh_ref[...], preferred_element_type=F32)
            acc = acc + jnp.dot(kl_ref[...], uh, preferred_element_type=F32)
            acc = acc + jnp.dot(kh_ref[...], ul, preferred_element_type=F32)
            ACC[b * zb : (b + 1) * zb] = acc.reshape(zb, X, Y)

    barrier = pltpu.get_barrier_semaphore()
    for axis, count in counts.items():
        for j in range(1, count):
            pl.semaphore_signal(barrier, inc=1, device_id={axis: peer(axis, j)}, device_id_type=MESH)

    own_x, own_y = xs(d), ys(c)
    V[pl.ds(s * owned, owned), own_x, own_y] = vel_ref[...]
    U[1, pl.ds(reach, depth), own_x, own_y] = now_ref[0].astype(F32)
    U[0, pl.ds(reach, depth), own_x, own_y] = prev_ref[0].astype(F32)
    SP[:, own_x, own_y] = sponge_ref[...].astype(F32)
    L[1, pl.ds(reach, depth), own_x, own_y] = adj_ref[0].astype(F32)
    L[0, pl.ds(reach, depth), own_x, own_y] = adjn_ref[0].astype(F32)

    pl.semaphore_wait(barrier, sum(counts.values()) - 3)

    vel_state = slab_send(in_slab(V), "dom", "shots")
    now_state = field_send(in_field(U, 1))
    sp_state = field_send(in_whole(SP))
    prev_state = field_send(in_field(U, 0))
    adj_state = field_send(in_field(L, 1))
    adjn_state = field_send(in_field(L, 0))

    edge = jnp.zeros((reach, X, Y), F32)
    for ref in (U, L):
        for n in range(ref.shape[0]):
            ref[n, 0:reach] = edge
            ref[n, reach + depth : 2 * reach + depth] = edge
    pos = rec_ref[...]
    row_of = jnp.zeros_like(pos)
    for x in range(1, X):
        row_of = row_of + (pos >= x * Y).astype(jnp.int32)
    col_of = pos - row_of * Y
    nrec = pos.shape[1]
    x_hot = (lax.broadcasted_iota(jnp.int32, (X, nrec), 0) == row_of).astype(F32)
    y_hot = (lax.broadcasted_iota(jnp.int32, (Y, nrec), 0) == col_of).astype(F32).astype(BF16)

    def spread(lhs):
        return lax.dot_general(lhs, y_hot, (((1,), (1,)), ((), ())), preferred_element_type=F32)

    CNT[...] = spread(x_hot.astype(BF16))
    slab_relay(in_slab(V), vel_state, "dom", "shots")
    for n in range(NF):
        vals = x_hot * obs_ref[0, n : n + 1, :]
        a = vals.astype(BF16)
        b, rest = split(vals - a.astype(F32))
        OB[n] = spread(a) + spread(b) + spread(rest)
    flat = lax.broadcasted_iota(jnp.int32, (X, Y), 0) * Y + lax.broadcasted_iota(jnp.int32, (X, Y), 1)
    src_hot = (flat == src_ref[0]).astype(F32)

    field_relay(in_field(U, 1), now_state)
    field_relay(in_whole(SP), sp_state)
    field_done(in_field(U, 1), now_state)
    lateral(U, 1)
    slab_relay_two(in_slab(V), vel_state, "dom", "shots")
    field_relay(in_field(U, 0), prev_state)
    slab_done(in_slab(V), vel_state, "dom", "shots")
    field_done(in_whole(SP), sp_state)
    for z in range(depth):
        damp = damp_rate * SP[z]
        inv = 1.0 / (1.0 + damp)
        IV[z] = inv
        QV[z] = (1.0 - damp) * inv
        vel = V[z]
        KP[z] = vel * vel * inv
    field_done(in_field(U, 0), prev_state)

    def level(ref, n, z, xr, yr, plane):
        mid = ref[n, reach + z, xr, yr]
        lap = ACC[z, xr, yr] + (3.0 * coeffs[0]) * mid
        for k in range(1, reach + 1):
            lap = lap + coeffs[k] * (ref[n, reach + z + k, xr, yr] + ref[n, reach + z - k, xr, yr])
        inv = IV[z, xr, yr]
        drive = 2.0 * mid if plane is None else 2.0 * mid + plane
        return inv * drive - QV[z, xr, yr] * ref[n - 1, reach + z, xr, yr] + KP[z, xr, yr] * lap

    whole_x, whole_y = slice(None), slice(None)

    def advance(ref, n, plane, at, ready=False):
        if not ready:
            lateral(ref, n)
        for z in range(depth):
            ref[n + 1, reach + z] = level(ref, n, z, whole_x, whole_y, plane if z == at else None)

    for n in range(NF):
        advance(U, n + 1, src_hot * amp_ref[0, n], src_depth, n == 0)
        if n == max(0, NF - 3):
            field_relay(in_field(L, 1), adj_state)
        if n == max(0, NF - 2):
            field_relay(in_field(L, 0), adjn_state)

    for z in range(depth):
        illum = None
        for n in range(NF):
            value = U[n + 2, reach + z, own_x, own_y]
            illum = value * value if illum is None else illum + value * value
        GI[1, z] = illum
    field_done(in_field(L, 1), adj_state)
    lateral(L, 1)
    far_first = sorted(range(1, shots), key=lambda j: -min(j, shots - j))

    def to_owners(f):
        return [
            (j, send(GI.at[f, pl.ds(peer("shots", j) * owned, owned)], GR.at[j - 1, f], "shots", j))
            for j in far_first
        ]

    illum_parts = to_owners(1)
    field_done(in_field(L, 0), adjn_state)

    for n in range(NF, 0, -1):
        plane = CNT[...] * U[n + 1, reach + rec_depth] - OB[n - 1]
        advance(L, NF + 1 - n, plane, rec_depth, n == NF)

    for z in range(depth):
        at = (reach + z, own_x, own_y)
        u = [U[(n,) + at] for n in range(NF + 2)]
        grad = None
        for n in range(NF):
            term = L[(NF + 1 - n,) + at] * (u[n + 2] - 2.0 * u[n + 1] + u[n])
            grad = term if grad is None else grad + term
        GI[0, z] = grad

    grad_parts = to_owners(0)
    lateral(U, NF + 1)
    below = GI[1, pl.ds(s * owned, owned)] + floor_share * shots
    for j, idx in illum_parts:
        arrived(idx, GR.at[j - 1, 1], "shots")
        below = below + GR[j - 1, 1]
    above = GI[0, pl.ds(s * owned, owned)]
    for j, idx in grad_parts:
        arrived(idx, GR.at[j - 1, 0], "shots")
        above = above + GR[j - 1, 0]
    mine = above / below
    PC[pl.ds(s * owned, owned), own_x, own_y] = mine
    pc_state = slab_send(in_slab(PC), "shots", "dom")
    slab_relay(in_slab(PC), pc_state, "shots", "dom")
    slab_relay_two(in_slab(PC), pc_state, "shots", "dom")
    slab_done(in_slab(PC), pc_state, "shots", "dom")
    top = jnp.abs(PC[0])
    for z in range(1, depth):
        top = jnp.maximum(top, jnp.abs(PC[z]))
    peak = jnp.max(jnp.max(top, axis=0, keepdims=True), axis=1, keepdims=True)
    scale = 1.0 / (peak + 1e-06)
    both_ref[0:owned] = mine * scale
    for z in range(depth):
        updated = V[z] * (1.0 - step_rate * (PC[z] * scale))
        KP[z] = updated * updated * IV[z]
    for n in range(NFIN):
        plane = src_hot * amp_ref[0, NF + n]
        if n > 0:
            lateral(U, NF + 1 + n)
        if n < NFIN - 1:
            for z in range(depth):
                U[NF + 2 + n, reach + z] = level(
                    U, NF + 1 + n, z, whole_x, whole_y, plane if z == src_depth else None
                )
        else:
            for z in range(depth):
                both_ref[owned + z] = level(U, NF + 1 + n, z, own_x, own_y, None)
            ACC[0] = plane * IV[src_depth]
            both_ref[owned + src_depth] += ACC[0, own_x, own_y]
    for copy in sent:
        copy.wait_send()


def part(both_ref, dir_ref, out_ref):
    owned = dir_ref.shape[0]
    dir_ref[...] = both_ref[0:owned]
    out_ref[0] = both_ref[owned:]


def solution(mesh):
    shots, dom, sub = mesh.shape["shots"], mesh.shape["dom"], mesh.shape["sub"]

    def shards(velocity, wave_prev, wave_now, adj_next, adj_now, sponge, wavelet, src_pos, rec_pos, observed):
        depth, rows, cols = sponge.shape
        owned = velocity.shape[0]
        X, Y = dom * rows, sub * cols
        zb = min(depth, max(1, 256 // X))
        bh, bl = band(Y, Y)
        kh, kl = band(zb * X, X)
        vm = pl.BlockSpec(memory_space=pltpu.VMEM)
        sm = pl.BlockSpec(memory_space=pltpu.SMEM)
        whole = pltpu.VMEM((depth, X, Y), F32)
        n_sems = copies_needed(shots, dom, sub)
        both = pl.pallas_call(
            functools.partial(kernel, (shots, dom, sub, depth, rows, cols, owned, zb)),
            out_shape=jax.ShapeDtypeStruct((owned + depth, rows, cols), F32),
            in_specs=[vm] * 6 + [sm, sm] + [vm] * 6,
            out_specs=vm,
            scratch_shapes=[
                pltpu.VMEM((NF + NFIN + 1, depth + 2 * reach, X, Y), F32),
                pltpu.VMEM((NF + 2, depth + 2 * reach, X, Y), F32),
                whole, whole, whole, whole, whole, whole, whole,
                pltpu.VMEM((NF, X, Y), F32),
                pltpu.VMEM((X, Y), F32),
                pltpu.VMEM((2, depth, rows, cols), F32),
                pltpu.VMEM((max(1, shots - 1), 2, owned, rows, cols), F32),
                pltpu.SemaphoreType.DMA((n_sems,)),
                pltpu.SemaphoreType.DMA((n_sems,)),
            ],
            compiler_params=pltpu.CompilerParams(
                collective_id=0, has_side_effects=True, vmem_limit_bytes=56 * 1024 * 1024
            ),
        )(velocity, wave_prev, wave_now, adj_next, adj_now, sponge, wavelet, src_pos, rec_pos, observed,
          jnp.asarray(bh), jnp.asarray(bl), jnp.asarray(kh), jnp.asarray(kl))
        return tuple(pl.pallas_call(
            part,
            out_shape=(
                jax.ShapeDtypeStruct((owned, rows, cols), F32),
                jax.ShapeDtypeStruct((1, depth, rows, cols), F32),
            ),
            in_specs=[vm],
            out_specs=(vm, vm),
        )(both))

    return jax.shard_map(
        shards,
        mesh=mesh,
        in_specs=(
            P(("groups", "shots"), "dom", "sub"),
            P(("groups", "shots"), None, "dom", "sub"),
            P(("groups", "shots"), None, "dom", "sub"),
            P(("groups", "shots"), None, "dom", "sub"),
            P(("groups", "shots"), None, "dom", "sub"),
            P(None, "dom", "sub"),
            P(("groups", "shots"), None),
            P(("groups", "shots")),
            P(("groups", "shots"), None),
            P(("groups", "shots"), None, None),
        ),
        out_specs=(
            P(("groups", "shots"), "dom", "sub"),
            P(("groups", "shots"), None, "dom", "sub"),
        ),
        check_vma=False,
    )
```
